256 devices in a mesh: row: 64 (over x, z_hi, y, core), col: 4 (over z_lo).
Axes of the slice: x: 4, y: 4, z: 8 (z_hi: 2, z_lo: 4; z = z_hi * 4 + z_lo), core: 2. Of those that a mesh axis runs over, the one named last changes fastest.
Arguments:
- matrix: float32 [32, 512, 8, 2048], P(None, 'row', None, 'col'), as said below
Outputs:
- factored: float32 [32, 512, 8, 2048], P(None, 'row', None, 'col')
Inputs may be any that keep to these rules, and one draw needn't show every extreme that they name: `matrix`: symmetric and positive definite.
All inputs are finite; a program needn't handle non-finite values.
Results may differ from the reference program's by a relative error of at most 0.0003.
Values sent between devices are 32-bit elements; how exact they have to be, the bound alone decides.
No kernel may reach another device: no remote copies, remote signals or barrier semaphores. Data moves between devices by JAX's collectives and lax.ppermute only.
A program may use at most 128 MiB of HBM per device.

```python
import math
import jax
import jax.numpy as jnp
from jax import lax

ORDER = 16384
CB = 512
RB = 8
PANELS = 2
LR = 32
LC = 8
N_ROW = 64
N_COL = 4


def draw_matrix(key, part):
    key_lower, key_diag, key_tail, key_noise, key_shift = jax.random.split(key, 5)
    matrix_order = ORDER
    lead_count = PANELS * CB
    rest_count = matrix_order - lead_count
    lower_raw = jax.random.normal(key_lower, (lead_count, lead_count), jnp.float32)
    tail_rows = jax.random.normal(key_tail, (rest_count, lead_count), jnp.float32)
    noise_draw = jax.random.normal(key_noise, (rest_count, rest_count), jnp.float32)
    diag_factor = jax.random.uniform(key_diag, (lead_count,), jnp.float32, 1.0, 2.0)
    lead_factor = jnp.tril(lower_raw, -1) * (0.4 / math.sqrt(lead_count)) + jnp.diag(diag_factor)
    stacked_factor = jnp.concatenate([lead_factor, tail_rows], axis=0)
    product = jnp.dot(stacked_factor, stacked_factor.T, precision=lax.Precision.HIGHEST, preferred_element_type=jnp.float32)
    product = (product + product.T) * 0.5
    sym_noise = (noise_draw + noise_draw.T) * (0.70710678 * 0.1)
    shift_values = 0.1 * math.sqrt(rest_count) * jax.random.uniform(key_shift, (rest_count,), jnp.float32, 2.5, 4.0)
    positions = jnp.arange(rest_count)
    sym_noise = sym_noise.at[positions, positions].set(shift_values)
    tail_block = product[lead_count:, lead_count:] + sym_noise
    assembled = product.at[lead_count:, lead_count:].set(tail_block)
    return assembled.reshape(LR, N_ROW * RB, LC, N_COL * CB)


def setup_inputs(seed: int = 0) -> dict:
    splits = jax.random.split(jax.random.key(seed), 2)
    matrix = draw_matrix(jax.random.fold_in(splits[1], 71), 0)
    return dict(matrix=matrix)


def reference(matrix):
    matrix_order = ORDER
    factored_count = PANELS * CB
    highest = lax.Precision.HIGHEST
    working = matrix.reshape(matrix_order, matrix_order)
    factor_columns = []
    for panel_number in range(PANELS):
        start_col = panel_number * CB
        stop_col = start_col + CB
        factor_block = jnp.linalg.cholesky(working[start_col:stop_col, start_col:stop_col])
        below_rows = jax.scipy.linalg.solve_triangular(factor_block, working[stop_col:, start_col:stop_col].T, lower=True).T
        product = jnp.dot(below_rows.astype(jnp.float32), below_rows.T.astype(jnp.float32), precision=highest, preferred_element_type=jnp.float32)
        working = working.at[stop_col:, stop_col:].set(working[stop_col:, stop_col:] - product)
        factor_column = jnp.concatenate([jnp.zeros((start_col, CB), jnp.float32), factor_block, below_rows], axis=0)
        factor_columns.append(factor_column)
    left_part = jnp.concatenate(factor_columns, axis=1)
    right_part = jnp.concatenate([jnp.zeros((factored_count, matrix_order - factored_count), jnp.float32), working[factored_count:, factored_count:]], axis=0)
    assembled = jnp.concatenate([left_part, right_part], axis=1)
    return assembled.reshape(LR, N_ROW * RB, LC, N_COL * CB)
```

```python
import functools

import jax
import jax.numpy as jnp
from jax import lax
from jax.experimental import pallas as pl
from jax.experimental.pallas import tpu as pltpu
from jax.sharding import PartitionSpec as P


W = 512
NB = 128
F32 = jnp.float32
HI = lax.Precision.HIGHEST
ANY = pl.BlockSpec(memory_space=pl.ANY)
VM = pl.BlockSpec(memory_space=pltpu.VMEM)
SM = pl.BlockSpec(memory_space=pltpu.SMEM)


def swap(value, mask, mask_odd=None):
    mask_odd = mask if mask_odd is None else mask_odd
    pairs = [(r, r ^ (mask_odd if r & 1 else mask)) for r in range(64)]
    return lax.ppermute(value, "row", pairs)


def dot(a, b, da=1, db=0):
    return lax.dot_general(
        a, b, (((da,), (db,)), ((), ())), precision=HI, preferred_element_type=F32
    )


def factor_block(load, store):
    lane = lax.broadcasted_iota(jnp.int32, (8, NB), 1)
    sub = lax.broadcasted_iota(jnp.int32, (8, NB), 0)
    left = [load(i) for i in range(16)]
    right = [jnp.where(lane == sub + 8 * i, F32(1), F32(0)) for i in range(16)]

    def lanes(v, j):
        return jnp.broadcast_to(v[:, j : j + 1], (8, NB))

    def subs(v, s):
        return jnp.broadcast_to(v[s : s + 1, :], (8, NB))

    for b in range(16):
        pa, pi = left[b], right[b]
        c = [lanes(pa, 8 * b + j) for j in range(8)]
        t = {(s, j): subs(c[j], s) for j in range(8) for s in range(j, 8)}
        rows_a = [subs(pa, s) for s in range(8)] if b < 15 else None
        rows_i = [subs(pi, s) for s in range(8)]
        r, d, m = [None] * 8, [None] * 8, {}
        for j in range(8):
            d[j] = t[j, j]
            r[j] = 1.0 / d[j]
            for s in range(j + 1, 8):
                m[s, j] = t[s, j] * r[j]
            for k in range(j + 1, 8):
                for s in range(k, 8):
                    t[s, k] = t[s, k] - m[s, j] * t[k, j]
        g = {}
        for s in range(8):
            for k in range(s):
                acc = -m[s, k]
                for q in range(k + 1, s):
                    acc = acc - m[s, q] * g[q, k]
                g[s, k] = acc

        def forward(rows):
            out = []
            for s in range(8):
                acc = rows[s]
                for k in range(s):
                    acc = acc + g[s, k] * rows[k]
                out.append(acc)
            return out

        def backward(rows):
            scaled = [r[s] * rows[s] for s in range(8)]
            out = []
            for j in range(8):
                acc = scaled[j]
                for s in range(j + 1, 8):
                    acc = acc + g[s, j] * scaled[s]
                out.append(acc)
            return out

        vi = forward(rows_i)
        if b < 15:
            wa, wi = backward(forward(rows_a)), backward(vi)
            for i in range(b + 1, 16):
                ci = [lanes(left[i], 8 * b + j) for j in range(8)]
                ta, ti = ci[0] * wa[0], ci[0] * wi[0]
                for j in range(1, 8):
                    ta, ti = ta + ci[j] * wa[j], ti + ci[j] * wi[j]
                left[i], right[i] = left[i] - ta, right[i] - ti
        out = lax.rsqrt(d[0]) * vi[0]
        for s in range(1, 8):
            out = jnp.where(sub == s, lax.rsqrt(d[s]) * vi[s], out)
        store(b, out)


def identity(work):
    row = lax.broadcasted_iota(jnp.int32, (W, W), 0)
    col = lax.broadcasted_iota(jnp.int32, (W, W), 1)
    work[:, W:] = jnp.where(row == col, F32(1), F32(0))


def factor_steps(work, inv, first, last):
    def step(kb, carry):
        top = pl.multiple_of(kb * NB, NB)
        nxt = pl.multiple_of((kb + 1) * NB, NB)

        def load(i):
            return work[pl.ds(top + 8 * i, 8), pl.ds(top, NB)]

        def store(i, v):
            inv[8 * i : 8 * i + 8, :] = v

        factor_block(load, store)
        work[pl.ds(top, NB), pl.ds(nxt, W)] = dot(
            inv[...], work[pl.ds(top, NB), pl.ds(nxt, W)]
        )

        def update(i, carry):
            at = pl.multiple_of(i * NB, NB)
            work[pl.ds(at, NB), pl.ds(nxt, W)] -= dot(
                work[pl.ds(top, NB), pl.ds(at, NB)],
                work[pl.ds(top, NB), pl.ds(nxt, W)],
                0,
                0,
            )
            return carry

        lax.fori_loop(kb + 1, W // NB, update, 0)
        return carry

    lax.fori_loop(first, last, step, 0)


def first_kernel(d00, work, inv):
    for x in range(4):
        for z in range(2):
            for y in range(8):
                at = 8 * (16 * x + 8 * z + y)
                work[at : at + 8, :W] = d00[8 * x + y, z]
    identity(work)
    factor_steps(work, inv, 0, 2)


def rest_kernel(part, full, work, inv):
    work[...] = part[...]
    factor_steps(work, inv, 2, 4)
    full[...] = work[:, W:]


def second_kernel(x0, d1, u01, work, d10, inv):
    for x in range(4):
        for z in range(2):
            for y in range(8):
                at = 8 * (16 * x + 8 * z + y)
                d10[at : at + 8, :] = d1[8 * x + y, z, 0]
                work[at : at + 8, :W] = d1[8 * x + y, z, 1]
    u01[...] = dot(x0[...], d10[...], 1, 1)
    work[:, :W] -= dot(u01[...], u01[...], 0, 0)
    identity(work)
    factor_steps(work, inv, 0, 2)


def own_rows_kernel(a0, a1, x0, x1, u01, b, g):
    b0 = dot(a0[...], x0[...], 1, 1)
    b1 = dot(a1[...] - dot(b0, u01[...]), x1[...], 1, 1)
    g1 = dot(b1, x1[...])
    b[:, :W] = b0
    b[:, W:] = b1
    g[:, W:] = g1
    g[:, :W] = dot(b0 - dot(g1, u01[...], 1, 1), x0[...])


def last_kernel(slots, place, pos, a, b, g, *rest):
    n = len(slots)
    bufs, out, held, sem = rest[:n], rest[n], rest[n + 1], rest[n + 2]
    for buf, ids in zip(bufs, slots):
        for at, slot in enumerate(ids):
            for l in range(2):
                pltpu.make_async_copy(buf.at[at, l], held.at[l, place[slot]], sem).start()
    pltpu.make_async_copy(held, held, sem).wait()
    r, c = pos[0], pos[1]
    row = lax.broadcasted_iota(jnp.int32, (256, W), 0)
    col = lax.broadcasted_iota(jnp.int32, (256, W), 1)
    held2 = held.reshape(1024 * 32, 128)

    def part(ref, m, n):
        return [ref[pl.ds(8 * t + m, n, stride=32), :] for t in range(4)]

    def one(m, carry):
        product = dot(g[...], jnp.concatenate(part(held2, m, 1024), axis=1))
        value = jnp.concatenate(part(a, m, 256), axis=1) - product
        trailing = (m > 0) | (c >= 2)
        value = jnp.where((row < 16) & trailing, F32(0), value)
        for t in range(4):
            out[pl.ds(8 * t + m, 256, stride=32), :] = value[:, 128 * t : 128 * t + 128]
        return carry

    lax.fori_loop(0, 8, one, 0)

    @pl.when(c < 2)
    def _():
        row_global = (row // 8) * W + r * 8 + row % 8
        mine = jnp.where(c == 0, b[:, :W], b[:, W:])
        value = jnp.where(row_global - c * W >= col, mine, F32(0))
        for t in range(4):
            out[pl.ds(8 * t, 256, stride=32), :] = value[:, 128 * t : 128 * t + 128]


def steps(matrix):
    r = lax.axis_index("row")
    c = lax.axis_index("col")
    z_hi = (r // 8) % 2
    tiles = matrix.reshape(256, 8, 4, 128).transpose(0, 2, 1, 3)
    own = matrix[:, :, 0, :].reshape(256, W)

    def by_col(value):
        def send(*pairs):
            return lax.ppermute(value, "col", list(pairs))

        s1 = send((0, 1), (1, 0))
        s2 = send((0, 2), (1, 3))
        s3 = send((0, 3), (1, 2))
        p0 = jnp.where(c == 0, value, jnp.where(c == 1, s1, jnp.where(c == 2, s2, s3)))
        p1 = jnp.where(c == 1, value, jnp.where(c == 0, s1, jnp.where(c == 3, s2, s3)))
        return p0, p1

    groups = [[q for q in range(64) if (q // 8) % 2 == z] for z in (0, 1)]

    def to_all(value):
        copies = jnp.broadcast_to(value, (32, *value.shape))
        return lax.all_to_all(
            copies, "row", split_axis=0, concat_axis=0, axis_index_groups=groups, tiled=True
        )

    d0, d1 = by_col(own[:16])
    mine = jnp.stack([d0[:8], d0[8:], d1[8:]])
    other = swap(mine, 8)
    both = jnp.where(z_hi == 0, jnp.stack([mine, other]), jnp.stack([other, mine]))
    d00 = to_all(both[:, 0])
    d1x = to_all(both[:, 1:])

    piece = tiles[:16].reshape(1, 2, 256, 128)
    t = jnp.concatenate([piece, swap(piece, 8)])
    a0, a1 = by_col(own)
    n1 = swap(t, 2, 16)
    n3 = swap(t, 6, 48)
    n2a = swap(n3[:1], 2, 16)
    n2b = swap(n1[1:], 6, 48)
    t = jnp.concatenate([t, n1, n2a, n2b, n3])
    m1 = swap(t, 16, 2)
    m3 = swap(t, 48, 6)
    m2a = swap(m3[:4], 16, 2)
    m2b = swap(m1[4:], 48, 6)
    bufs = [t, m1, m2a, m2b, m3]
    base = [(q, z) for q in range(4) for z in (0, 8)]
    tags = [
        [(p, q, z, 0) for q, z in part]
        for p, part in [(0, base), (1, base), (2, base[:4]), (2, base[4:]), (3, base)]
    ]
    for v in list(bufs):
        bufs.append(swap(v, 1))
    tags += [[(p, q, z, 1) for p, q, z, _ in tag] for tag in tags]
    flat = [tag for part in tags for tag in part]
    index = {tag: i for i, tag in enumerate(flat)}
    slots = [[index[tag] for tag in part] for part in tags]
    even = jnp.array([16 * p + 2 * q + z + k for p, q, z, k in flat], jnp.int32)
    odd = jnp.array([16 * q + 2 * p + z + k for p, q, z, k in flat], jnp.int32)
    crossed = jnp.array([k for _, _, _, k in flat], jnp.int32)
    parity = (r + crossed) % 2
    place = jnp.bitwise_xor(jnp.where(parity == 1, odd, even), r).astype(jnp.int32)
    pos = jnp.stack([r, c]).astype(jnp.int32)

    square = jax.ShapeDtypeStruct((W, W), F32)
    double = jax.ShapeDtypeStruct((W, 2 * W), F32)
    inv = pltpu.VMEM((NB, NB), F32)
    work = pltpu.VMEM((W, 2 * W), F32)
    rest = pl.pallas_call(
        rest_kernel, out_shape=square, in_specs=[VM], out_specs=VM, scratch_shapes=[work, inv]
    )
    part0 = pl.pallas_call(
        first_kernel, out_shape=double, in_specs=[VM], out_specs=VM, scratch_shapes=[inv]
    )(d00)
    x0 = rest(part0)
    u01, part1 = pl.pallas_call(
        second_kernel,
        out_shape=[square, double],
        in_specs=[VM] * 2,
        out_specs=[VM] * 2,
        scratch_shapes=[pltpu.VMEM((W, W), F32), inv],
    )(x0, d1x)
    x1 = rest(part1)
    wide = jax.ShapeDtypeStruct((256, 2 * W), F32)
    b, g = pl.pallas_call(
        own_rows_kernel, out_shape=[wide, wide], in_specs=[VM] * 5, out_specs=[VM] * 2
    )(a0, a1, x0, x1, u01)
    result = pl.pallas_call(
        functools.partial(last_kernel, slots),
        out_shape=jax.ShapeDtypeStruct((8192, 128), F32),
        in_specs=[SM, SM, VM, VM, VM] + [ANY] * len(bufs),
        out_specs=VM,
        scratch_shapes=[pltpu.VMEM((2, 64, 256, 128), F32), pltpu.SemaphoreType.DMA],
    )(place, pos, tiles.reshape(8192, 128), b, g, *bufs)
    return result.reshape(256, 4, 8, 128).transpose(0, 2, 1, 3).reshape(matrix.shape)


def solution(mesh):
    return jax.shard_map(
        steps,
        mesh=mesh,
        in_specs=(P(None, "row", None, "col"),),
        out_specs=P(None, "row", None, "col"),
        check_vma=False,
    )
```

```python
import functools

import jax
import jax.numpy as jnp
from jax import lax
from jax.experimental import pallas as pl
from jax.experimental.pallas import tpu as pltpu
from jax.sharding import PartitionSpec as P


W = 512
NB = 128
F32 = jnp.float32
HI = lax.Precision.HIGHEST
ANY = pl.BlockSpec(memory_space=pl.ANY)
VM = pl.BlockSpec(memory_space=pltpu.VMEM)
SM = pl.BlockSpec(memory_space=pltpu.SMEM)


def swap(value, mask, mask_odd=None):
    mask_odd = mask if mask_odd is None else mask_odd
    pairs = [(r, r ^ (mask_odd if r & 1 else mask)) for r in range(64)]
    return lax.ppermute(value, "row", pairs)


def dot(a, b, da=1, db=0):
    return lax.dot_general(
        a, b, (((da,), (db,)), ((), ())), precision=HI, preferred_element_type=F32
    )


def total(terms):
    while len(terms) > 1:
        pairs = [terms[i] + terms[i + 1] for i in range(0, len(terms) - 1, 2)]
        terms = pairs + terms[2 * len(pairs) :]
    return terms[0]


def factor_block(load, store):
    lane = lax.broadcasted_iota(jnp.int32, (8, NB), 1)
    sub = lax.broadcasted_iota(jnp.int32, (8, NB), 0)
    left = [load(i) for i in range(16)]
    right = [jnp.where(lane == sub + 8 * i, F32(1), F32(0)) for i in range(16)]

    def lanes(v, j):
        return jnp.broadcast_to(v[:, j : j + 1], (8, NB))

    def subs(v, s):
        return jnp.broadcast_to(v[s : s + 1, :], (8, NB))

    for b in range(16):
        more = b < 15
        c = [lanes(left[b], 8 * b + j) for j in range(8)]
        t = {(s, j): subs(c[j], s) for j in range(8) for s in range(j, 8)}
        va = [subs(left[b], s) for s in range(8)] if more else None
        vi = [subs(right[b], s) for s in range(8)]
        nx = [lanes(left[b + 1], 8 * b + j) for j in range(8)] if more else None
        r, d, m = [None] * 8, [None] * 8, {}
        for j in range(8):
            d[j] = t[j, j]
            r[j] = 1.0 / d[j]
            for s in range(j + 1, 8):
                m[s, j] = t[s, j] * r[j]
            for k in range(j + 1, 8):
                for s in range(k, 8):
                    t[s, k] = t[s, k] - m[s, j] * t[k, j]
            for s in range(j + 1, 8):
                if more:
                    va[s] = va[s] - m[s, j] * va[j]
                    nx[s] = nx[s] - m[s, j] * nx[j]
                vi[s] = vi[s] - m[s, j] * vi[j]
        if more:
            wa = [r[s] * va[s] for s in range(8)]
            wi = [r[s] * vi[s] for s in range(8)]
            next_left = left[b + 1] - total([nx[j] * wa[j] for j in range(8)])
            next_right = right[b + 1] - total([nx[j] * wi[j] for j in range(8)])
            for s in range(7, 0, -1):
                for j in range(s):
                    wa[j] = wa[j] - m[s, j] * wa[s]
                    wi[j] = wi[j] - m[s, j] * wi[s]
            for i in range(b + 2, 16):
                ci = [lanes(left[i], 8 * b + j) for j in range(8)]
                left[i] = left[i] - total([ci[j] * wa[j] for j in range(8)])
                right[i] = right[i] - total([ci[j] * wi[j] for j in range(8)])
            left[b + 1], right[b + 1] = next_left, next_right
        out = lax.rsqrt(d[0]) * vi[0]
        for s in range(1, 8):
            out = jnp.where(sub == s, lax.rsqrt(d[s]) * vi[s], out)
        store(b, out)


def identity(work):
    row = lax.broadcasted_iota(jnp.int32, (W, W), 0)
    col = lax.broadcasted_iota(jnp.int32, (W, W), 1)
    work[:, W:] = jnp.where(row == col, F32(1), F32(0))


def factor_steps(work, inv, first, last):
    def step(kb, carry):
        top = pl.multiple_of(kb * NB, NB)
        nxt = pl.multiple_of((kb + 1) * NB, NB)

        def load(i):
            return work[pl.ds(top + 8 * i, 8), pl.ds(top, NB)]

        def store(i, v):
            inv[8 * i : 8 * i + 8, :] = v

        factor_block(load, store)
        work[pl.ds(top, NB), pl.ds(nxt, W)] = dot(
            inv[...], work[pl.ds(top, NB), pl.ds(nxt, W)]
        )

        def update(i, carry):
            at = pl.multiple_of(i * NB, NB)
            work[pl.ds(at, NB), pl.ds(nxt, W)] -= dot(
                work[pl.ds(top, NB), pl.ds(at, NB)],
                work[pl.ds(top, NB), pl.ds(nxt, W)],
                0,
                0,
            )
            return carry

        lax.fori_loop(kb + 1, W // NB, update, 0)
        return carry

    lax.fori_loop(first, last, step, 0)


def first_kernel(d00, work, inv):
    for x in range(4):
        for z in range(2):
            for y in range(8):
                at = 8 * (16 * x + 8 * z + y)
                work[at : at + 8, :W] = d00[8 * x + y, z]
    identity(work)
    factor_steps(work, inv, 0, 2)


def rest_kernel(part, full, work, inv):
    work[W // 2 :, :] = part[W // 2 :, :]
    factor_steps(work, inv, 2, 4)
    full[: W // 2, :] = part[: W // 2, W:]
    full[W // 2 :, :] = work[W // 2 :, W:]


def second_kernel(x0, d1, u01, work, d10, inv):
    for x in range(4):
        for z in range(2):
            for y in range(8):
                at = 8 * (16 * x + 8 * z + y)
                d10[at : at + 8, :] = d1[8 * x + y, z, 0]
                work[at : at + 8, :W] = d1[8 * x + y, z, 1]
    u01[...] = dot(x0[...], d10[...], 1, 1)
    work[:, :W] -= dot(u01[...], u01[...], 0, 0)
    identity(work)
    factor_steps(work, inv, 0, 2)


def own_rows_kernel(a0, a1, x0, x1, u01, b, g):
    b0 = dot(a0[...], x0[...], 1, 1)
    b1 = dot(a1[...] - dot(b0, u01[...]), x1[...], 1, 1)
    g1 = dot(b1, x1[...])
    b[:, :W] = b0
    b[:, W:] = b1
    g[:, W:] = g1
    g[:, :W] = dot(b0 - dot(g1, u01[...], 1, 1), x0[...])


def thirds(v):
    high = v.astype(jnp.bfloat16)
    rest = v - high.astype(F32)
    mid = rest.astype(jnp.bfloat16)
    return high, mid, (rest - mid.astype(F32)).astype(jnp.bfloat16)


def bdot(a, b):
    return lax.dot_general(a, b, (((1,), (0,)), ((), ())), preferred_element_type=F32)


def last_kernel(slots, place, pos, a, b, g, *rest):
    n = len(slots)
    bufs, out, (held, tile, parts, held_sem, in_sem, out_sem) = rest[:n], rest[n], rest[n + 1 :]
    r, c = pos[0], pos[1]
    for t in range(4):
        for buf, ids in zip(bufs, slots):
            for at, slot in enumerate(ids):
                for l in range(2):
                    row = pl.multiple_of(8 * (64 * l + place[slot]), 8)
                    pltpu.make_async_copy(
                        buf.at[at, l, :, pl.ds(1024 * t, 1024)],
                        held.at[t, pl.ds(row, 8)],
                        held_sem.at[t],
                    ).start()
        pltpu.make_async_copy(a.at[:, t], tile.at[t], in_sem.at[t]).start()
    for k, v in enumerate(thirds(g[...])):
        parts[k] = v
    row = lax.broadcasted_iota(jnp.int32, (256, 128), 0)
    col = lax.broadcasted_iota(jnp.int32, (256, 128), 1)
    row_global = (row // 8) * W + r * 8 + row % 8
    for t in range(4):
        pltpu.make_async_copy(held.at[t], held.at[t], held_sem.at[t]).wait()
        pltpu.make_async_copy(tile.at[t], tile.at[t], in_sem.at[t]).wait()
        flat = tile.at[t].reshape(2048, 128)

        def some(i, carry):
            high, mid, low = thirds(held[t, :, pl.ds(pl.multiple_of(512 * i, 512), 512)])
            product = (
                bdot(parts[0], low)
                + bdot(parts[2], high)
                + bdot(parts[1], mid)
                + bdot(parts[0], mid)
                + bdot(parts[1], high)
                + bdot(parts[0], high)
            )
            for k in range(4):
                m = 4 * i + k
                at = pl.ds(m, 256, stride=8)
                value = flat[at, :] - product[:, 128 * k : 128 * k + 128]
                trailing = (m > 0) | (c >= 2)
                flat[at, :] = jnp.where((row < 16) & trailing, F32(0), value)
            return carry

        lax.fori_loop(0, 2, some, 0)

        @pl.when(c < 2)
        def _():
            first, second = b[:, 128 * t : 128 * t + 128], b[:, W + 128 * t : W + 128 * t + 128]
            mine = jnp.where(c == 0, first, second)
            flat[pl.ds(0, 256, stride=8), :] = jnp.where(
                row_global - c * W >= col + 128 * t, mine, F32(0)
            )

        pltpu.make_async_copy(tile.at[t], out.at[:, t], out_sem.at[t]).start()
    for t in range(4):
        pltpu.make_async_copy(tile.at[t], out.at[:, t], out_sem.at[t]).wait()


def steps(matrix):
    r = lax.axis_index("row")
    c = lax.axis_index("col")
    z_hi = (r // 8) % 2
    tiles = matrix.reshape(256, 8, 4, 128).transpose(0, 2, 1, 3)
    own = matrix[:, :, 0, :].reshape(256, W)

    def by_col(value):
        def send(*pairs):
            return lax.ppermute(value, "col", list(pairs))

        s1 = send((0, 1), (1, 0))
        s2 = send((0, 2), (1, 3))
        s3 = send((0, 3), (1, 2))
        p0 = jnp.where(c == 0, value, jnp.where(c == 1, s1, jnp.where(c == 2, s2, s3)))
        p1 = jnp.where(c == 1, value, jnp.where(c == 0, s1, jnp.where(c == 3, s2, s3)))
        return p0, p1

    groups = [[q for q in range(64) if (q // 8) % 2 == z] for z in (0, 1)]

    def to_all(value):
        copies = jnp.broadcast_to(value, (32, *value.shape))
        return lax.all_to_all(
            copies, "row", split_axis=0, concat_axis=0, axis_index_groups=groups, tiled=True
        )

    d0, d1 = by_col(own[:16])
    mine = jnp.stack([d0[:8], d0[8:], d1[8:]])
    other = swap(mine, 8)
    both = jnp.where(z_hi == 0, jnp.stack([mine, other]), jnp.stack([other, mine]))
    d00 = to_all(both[:, 0])
    d1x = to_all(both[:, 1:])

    piece = tiles[:16].reshape(2, 8, 4096).reshape(1, 2, 8, 4096)
    t = jnp.concatenate([piece, swap(piece, 8)])
    a0, a1 = by_col(own)
    n1 = swap(t, 2, 16)
    n3 = swap(t, 6, 48)
    n2 = swap(n3, 2, 16)
    t = jnp.concatenate([t, n1, n2, n3])
    m1 = swap(t, 16, 2)
    m3 = swap(t, 48, 6)
    m2 = swap(m3, 16, 2)
    bufs = [t, m1, m2, m3]
    base = [(q, z) for q in range(4) for z in (0, 8)]
    tags = [[(p, q, z, 0) for q, z in base] for p in range(4)]
    for v in list(bufs):
        bufs.append(swap(v, 1))
    tags += [[(p, q, z, 1) for p, q, z, _ in tag] for tag in tags]
    flat = [tag for part in tags for tag in part]
    index = {tag: i for i, tag in enumerate(flat)}
    slots = [[index[tag] for tag in part] for part in tags]
    even = jnp.array([16 * p + 2 * q + z + k for p, q, z, k in flat], jnp.int32)
    odd = jnp.array([16 * q + 2 * p + z + k for p, q, z, k in flat], jnp.int32)
    crossed = jnp.array([k for _, _, _, k in flat], jnp.int32)
    parity = (r + crossed) % 2
    place = jnp.bitwise_xor(jnp.where(parity == 1, odd, even), r).astype(jnp.int32)
    pos = jnp.stack([r, c]).astype(jnp.int32)

    square = jax.ShapeDtypeStruct((W, W), F32)
    double = jax.ShapeDtypeStruct((W, 2 * W), F32)
    inv = pltpu.VMEM((NB, NB), F32)
    work = pltpu.VMEM((W, 2 * W), F32)
    rest = pl.pallas_call(
        rest_kernel, out_shape=square, in_specs=[VM], out_specs=VM, scratch_shapes=[work, inv]
    )
    part0 = pl.pallas_call(
        first_kernel, out_shape=double, in_specs=[VM], out_specs=VM, scratch_shapes=[inv]
    )(d00)
    x0 = rest(part0)
    u01, part1 = pl.pallas_call(
        second_kernel,
        out_shape=[square, double],
        in_specs=[VM] * 2,
        out_specs=[VM] * 2,
        scratch_shapes=[pltpu.VMEM((W, W), F32), inv],
    )(x0, d1x)
    x1 = rest(part1)
    wide = jax.ShapeDtypeStruct((256, 2 * W), F32)
    b, g = pl.pallas_call(
        own_rows_kernel, out_shape=[wide, wide], in_specs=[VM] * 5, out_specs=[VM] * 2
    )(a0, a1, x0, x1, u01)
    result = pl.pallas_call(
        functools.partial(last_kernel, slots),
        out_shape=jax.ShapeDtypeStruct((256, 4, 8, 128), F32),
        in_specs=[SM, SM, ANY, VM, VM] + [ANY] * len(bufs),
        out_specs=ANY,
        scratch_shapes=[
            pltpu.VMEM((4, 1024, 1024), F32),
            pltpu.VMEM((4, 256, 8, 128), F32),
            pltpu.VMEM((3, 256, 1024), jnp.bfloat16),
            pltpu.SemaphoreType.DMA((4,)),
            pltpu.SemaphoreType.DMA((4,)),
            pltpu.SemaphoreType.DMA((4,)),
        ],
    )(place, pos, tiles, b, g, *bufs)
    return result.transpose(0, 2, 1, 3).reshape(matrix.shape)


def solution(mesh):
    return jax.shard_map(
        steps,
        mesh=mesh,
        in_specs=(P(None, "row", None, "col"),),
        out_specs=P(None, "row", None, "col"),
        check_vma=False,
    )
```

```python
import functools

import jax
import jax.numpy as jnp
from jax import lax
from jax.experimental import pallas as pl
from jax.experimental.pallas import tpu as pltpu
from jax.sharding import PartitionSpec as P


W = 512
NB = 128
F32 = jnp.float32
HI = lax.Precision.HIGHEST
ANY = pl.BlockSpec(memory_space=pl.ANY)
VM = pl.BlockSpec(memory_space=pltpu.VMEM)


def swap(value, mask, mask_odd=None):
    mask_odd = mask if mask_odd is None else mask_odd
    pairs = [(r, r ^ (mask_odd if r & 1 else mask)) for r in range(64)]
    return lax.ppermute(value, "row", pairs)


def dot(a, b, da=1, db=0):
    return lax.dot_general(
        a, b, (((da,), (db,)), ((), ())), precision=HI, preferred_element_type=F32
    )


def total(terms):
    while len(terms) > 1:
        pairs = [terms[i] + terms[i + 1] for i in range(0, len(terms) - 1, 2)]
        terms = pairs + terms[2 * len(pairs) :]
    return terms[0]


def factor_block(load, store):
    lane = lax.broadcasted_iota(jnp.int32, (8, NB), 1)
    sub = lax.broadcasted_iota(jnp.int32, (8, NB), 0)
    left = [load(i) for i in range(16)]
    right = [jnp.where(lane == sub + 8 * i, F32(1), F32(0)) for i in range(16)]

    def lanes(v, j):
        return jnp.broadcast_to(v[:, j : j + 1], (8, NB))

    def subs(v, s):
        return jnp.broadcast_to(v[s : s + 1, :], (8, NB))

    for b in range(16):
        more = b < 15
        c = [lanes(left[b], 8 * b + j) for j in range(8)]
        t = {(s, j): subs(c[j], s) for j in range(8) for s in range(j, 8)}
        va = [subs(left[b], s) for s in range(8)] if more else None
        vi = [subs(right[b], s) for s in range(8)]
        nx = [lanes(left[b + 1], 8 * b + j) for j in range(8)] if more else None
        r, d, m = [None] * 8, [None] * 8, {}
        for j in range(8):
            d[j] = t[j, j]
            r[j] = 1.0 / d[j]
            for s in range(j + 1, 8):
                m[s, j] = t[s, j] * r[j]
            for k in range(j + 1, 8):
                for s in range(k, 8):
                    t[s, k] = t[s, k] - m[s, j] * t[k, j]
            for s in range(j + 1, 8):
                if more:
                    va[s] = va[s] - m[s, j] * va[j]
                    nx[s] = nx[s] - m[s, j] * nx[j]
                vi[s] = vi[s] - m[s, j] * vi[j]
        if more:
            wa = [r[s] * va[s] for s in range(8)]
            wi = [r[s] * vi[s] for s in range(8)]
            next_left = left[b + 1] - total([nx[j] * wa[j] for j in range(8)])
            next_right = right[b + 1] - total([nx[j] * wi[j] for j in range(8)])
            for s in range(7, 0, -1):
                for j in range(s):
                    wa[j] = wa[j] - m[s, j] * wa[s]
                    wi[j] = wi[j] - m[s, j] * wi[s]
            for i in range(b + 2, 16):
                ci = [lanes(left[i], 8 * b + j) for j in range(8)]
                left[i] = left[i] - total([ci[j] * wa[j] for j in range(8)])
                right[i] = right[i] - total([ci[j] * wi[j] for j in range(8)])
            left[b + 1], right[b + 1] = next_left, next_right
        out = lax.rsqrt(d[0]) * vi[0]
        for s in range(1, 8):
            out = jnp.where(sub == s, lax.rsqrt(d[s]) * vi[s], out)
        store(b, out)


def identity(work):
    row = lax.broadcasted_iota(jnp.int32, (W, W), 0)
    col = lax.broadcasted_iota(jnp.int32, (W, W), 1)
    work[:, W:] = jnp.where(row == col, F32(1), F32(0))


def factor_steps(work, inv, first, last):
    def step(kb, carry):
        top = pl.multiple_of(kb * NB, NB)
        nxt = pl.multiple_of((kb + 1) * NB, NB)

        def load(i):
            return work[pl.ds(top + 8 * i, 8), pl.ds(top, NB)]

        def store(i, v):
            inv[8 * i : 8 * i + 8, :] = v

        factor_block(load, store)
        work[pl.ds(top, NB), pl.ds(nxt, W)] = dot(
            inv[...], work[pl.ds(top, NB), pl.ds(nxt, W)]
        )

        def update(i, carry):
            at = pl.multiple_of(i * NB, NB)
            work[pl.ds(at, NB), pl.ds(nxt, W)] -= dot(
                work[pl.ds(top, NB), pl.ds(at, NB)],
                work[pl.ds(top, NB), pl.ds(nxt, W)],
                0,
                0,
            )
            return carry

        lax.fori_loop(kb + 1, W // NB, update, 0)
        return carry

    lax.fori_loop(first, last, step, 0)


def lay_out(work, cols, own, other, part):
    core = lax.axis_index("row") % 2
    for x in range(4):
        for y in range(4):
            for z in range(2):
                for source, k in ((own, core), (other, 1 - core)):
                    at = pl.multiple_of(8 * (16 * x + 8 * z + 2 * y + k), 8)
                    work[pl.ds(at, 8), cols] = source[4 * x + y, z, part]


def first_kernel(own, other, x0, work, inv):
    lay_out(work, slice(0, W), own, other, 0)
    identity(work)
    factor_steps(work, inv, 0, 4)
    x0[...] = work[:, W:]


def second_kernel(x0, own, other, u01, x1, work, inv):
    lay_out(work, slice(W, 2 * W), own, other, 0)
    lay_out(work, slice(0, W), own, other, 1)
    u01[...] = dot(x0[...], work[:, W:], 1, 1)
    work[:, :W] -= dot(u01[...], u01[...], 0, 0)
    identity(work)
    factor_steps(work, inv, 0, 4)
    x1[...] = work[:, W:]


def own_rows_kernel(x0, x1, u01, own, s1, s2, s3, b, g, a0, a1, sem):
    c = lax.axis_index("col")
    for dst, sources, k in ((a0, (own, s1, s2, s3), 0), (a1, (s1, own, s3, s2), 1)):
        for i, source in enumerate(sources):

            @pl.when(c == i)
            def _():
                pltpu.make_async_copy(source, dst, sem.at[k]).start()

        pltpu.make_async_copy(own, dst, sem.at[k]).wait()
    b0 = dot(a0[...], x0[...], 1, 1)
    b1 = dot(a1[...] - dot(b0, u01[...]), x1[...], 1, 1)
    g1 = dot(b1, x1[...])
    b[:, :W] = b0
    b[:, W:] = b1
    g[:, W:] = g1
    g[:, :W] = dot(b0 - dot(g1, u01[...], 1, 1), x0[...])


def thirds(v):
    high = v.astype(jnp.bfloat16)
    rest = v - high.astype(F32)
    mid = rest.astype(jnp.bfloat16)
    return high, mid, (rest - mid.astype(F32)).astype(jnp.bfloat16)


def bdot(a, b):
    return lax.dot_general(a, b, (((1,), (0,)), ((), ())), preferred_element_type=F32)


def last_kernel(slots, a, b, g, *rest):
    n = len(slots)
    bufs, out, (held, tile, parts, held_sem, in_sem, out_sem) = rest[:n], rest[n], rest[n + 1 :]
    r, c = lax.axis_index("row"), lax.axis_index("col")
    place = [
        [jnp.bitwise_xor(r, jnp.where((r + k) % 2 == 1, odd, even)) for even, odd, k in ids]
        for ids in slots
    ]

    def fetch(t, carry):
        columns = pl.ds(pl.multiple_of(1024 * t, 1024), 1024)
        for buf, rows in zip(bufs, place):
            for at, block in enumerate(rows):
                for l in range(2):
                    row = pl.multiple_of(8 * (64 * l + block), 8)
                    pltpu.make_async_copy(
                        buf.at[at, l, :, columns], held.at[t, pl.ds(row, 8)], held_sem.at[t]
                    ).start()
        pltpu.make_async_copy(a.at[:, t], tile.at[t], in_sem.at[t]).start()
        return carry

    lax.fori_loop(0, 4, fetch, 0)
    for k, v in enumerate(thirds(g[...])):
        parts[k] = v
    row = lax.broadcasted_iota(jnp.int32, (256, 128), 0)
    col = lax.broadcasted_iota(jnp.int32, (256, 128), 1)
    row_global = (row // 8) * W + r * 8 + row % 8

    def column(t, carry):
        pltpu.make_async_copy(held.at[t], held.at[t], held_sem.at[t]).wait()
        pltpu.make_async_copy(tile.at[t], tile.at[t], in_sem.at[t]).wait()
        flat = tile.at[t].reshape(2048, 128)

        def some(i, carry):
            high, mid, low = thirds(held[t, :, pl.ds(pl.multiple_of(512 * i, 512), 512)])
            product = (
                bdot(parts[0], low)
                + bdot(parts[2], high)
                + bdot(parts[1], mid)
                + bdot(parts[0], mid)
                + bdot(parts[1], high)
                + bdot(parts[0], high)
            )
            for k in range(4):
                m = 4 * i + k
                at = pl.ds(m, 256, stride=8)
                value = flat[at, :] - product[:, 128 * k : 128 * k + 128]
                trailing = (m > 0) | (c >= 2)
                flat[at, :] = jnp.where((row < 16) & trailing, F32(0), value)
            return carry

        lax.fori_loop(0, 2, some, 0)

        @pl.when(c < 2)
        def _():
            at = pl.ds(pl.multiple_of(128 * t, 128), 128)
            ahead = pl.ds(pl.multiple_of(W + 128 * t, 128), 128)
            first, second = b[:, at], b[:, ahead]
            mine = jnp.where(c == 0, first, second)
            flat[pl.ds(0, 256, stride=8), :] = jnp.where(
                row_global - c * W >= col + 128 * t, mine, F32(0)
            )

        pltpu.make_async_copy(tile.at[t], out.at[:, t], out_sem.at[t]).start()
        return carry

    lax.fori_loop(0, 4, column, 0)
    for t in range(4):
        pltpu.make_async_copy(tile.at[t], out.at[:, t], out_sem.at[t]).wait()


def steps(matrix):
    r = lax.axis_index("row")
    c = lax.axis_index("col")
    z_hi = (r // 8) % 2
    tiles = matrix.reshape(256, 8, 4, 128).transpose(0, 2, 1, 3)
    own = matrix[:, :, 0, :].reshape(256, W)

    def by_col(value):
        def send(*pairs):
            return lax.ppermute(value, "col", list(pairs))

        return send((0, 1), (1, 0)), send((0, 2), (1, 3)), send((0, 3), (1, 2))

    groups = [
        [q for q in range(64) if (q // 8) % 2 == z and q % 2 == k] for z in (0, 1) for k in (0, 1)
    ]

    def to_all(value):
        copies = jnp.broadcast_to(value, (16, *value.shape))
        return lax.all_to_all(
            copies, "row", split_axis=0, concat_axis=0, axis_index_groups=groups, tiled=True
        )

    head = own[:16]
    s1, s2, s3 = by_col(head)
    d0 = jnp.where(c == 0, head, jnp.where(c == 1, s1, jnp.where(c == 2, s2, s3)))
    d1 = jnp.where(c == 1, head, jnp.where(c == 0, s1, jnp.where(c == 3, s2, s3)))
    mine = jnp.stack([d0[:8], d0[8:], d1[8:]])
    other = swap(mine, 8)
    both = jnp.where(z_hi == 0, jnp.stack([mine, other]), jnp.stack([other, mine]))
    d00 = to_all(both[:, :1])
    d00_other = swap(d00, 1)
    d1x = to_all(both[:, 1:])
    d1x_other = swap(d1x, 1)

    piece = tiles[:16].reshape(2, 8, 4096).reshape(1, 2, 8, 4096)
    t = jnp.concatenate([piece, swap(piece, 8)])
    a1, a2, a3 = by_col(own)
    n1 = swap(t, 2, 16)
    n3 = swap(t, 6, 48)
    n2 = swap(n3, 2, 16)
    t = jnp.concatenate([t, n1, n2, n3])
    m1 = swap(t, 16, 2)
    m3 = swap(t, 48, 6)
    m2 = swap(m3, 16, 2)
    bufs = [t, m1, m2, m3]
    for v in list(bufs):
        bufs.append(swap(v, 1))
    slots = [
        [(16 * p + 2 * q + z + k, 16 * q + 2 * p + z + k, k) for q in range(4) for z in (0, 8)]
        for k in (0, 1)
        for p in range(4)
    ]

    square = jax.ShapeDtypeStruct((W, W), F32)
    wide = jax.ShapeDtypeStruct((256, 2 * W), F32)
    scratch = [pltpu.VMEM((W, 2 * W), F32), pltpu.VMEM((NB, NB), F32)]
    x0 = pl.pallas_call(
        first_kernel, out_shape=square, in_specs=[VM] * 2, out_specs=VM, scratch_shapes=scratch
    )(d00, d00_other)
    u01, x1 = pl.pallas_call(
        second_kernel,
        out_shape=[square, square],
        in_specs=[VM] * 3,
        out_specs=[VM] * 2,
        scratch_shapes=scratch,
    )(x0, d1x, d1x_other)
    b, g = pl.pallas_call(
        own_rows_kernel,
        out_shape=[wide, wide],
        in_specs=[VM] * 3 + [ANY] * 4,
        out_specs=[VM] * 2,
        scratch_shapes=[
            pltpu.VMEM((256, W), F32),
            pltpu.VMEM((256, W), F32),
            pltpu.SemaphoreType.DMA((2,)),
        ],
    )(x0, x1, u01, own, a1, a2, a3)
    result = pl.pallas_call(
        functools.partial(last_kernel, slots),
        out_shape=jax.ShapeDtypeStruct((256, 4, 8, 128), F32),
        in_specs=[ANY, VM, VM] + [ANY] * len(bufs),
        out_specs=ANY,
        scratch_shapes=[
            pltpu.VMEM((4, 1024, 1024), F32),
            pltpu.VMEM((4, 256, 8, 128), F32),
            pltpu.VMEM((3, 256, 1024), jnp.bfloat16),
            pltpu.SemaphoreType.DMA((4,)),
            pltpu.SemaphoreType.DMA((4,)),
            pltpu.SemaphoreType.DMA((4,)),
        ],
    )(tiles, b, g, *bufs)
    return result.transpose(0, 2, 1, 3).reshape(matrix.shape)


def solution(mesh):
    return jax.shard_map(
        steps,
        mesh=mesh,
        in_specs=(P(None, "row", None, "col"),),
        out_specs=P(None, "row", None, "col"),
        check_vma=False,
    )
```

```python
import functools

import jax
import jax.numpy as jnp
from jax import lax
from jax.experimental import pallas as pl
from jax.experimental.pallas import tpu as pltpu
from jax.sharding import PartitionSpec as P


W = 512
NB = 128
F32 = jnp.float32
HI = lax.Precision.HIGHEST
ANY = pl.BlockSpec(memory_space=pl.ANY)
VM = pl.BlockSpec(memory_space=pltpu.VMEM)


def swap(value, mask, mask_odd=None):
    mask_odd = mask if mask_odd is None else mask_odd
    pairs = [(r, r ^ (mask_odd if r & 1 else mask)) for r in range(64)]
    return lax.ppermute(value, "row", pairs)


def dot(a, b, da=1, db=0):
    return lax.dot_general(
        a, b, (((da,), (db,)), ((), ())), precision=HI, preferred_element_type=F32
    )


def total(terms):
    while len(terms) > 1:
        pairs = [terms[i] + terms[i + 1] for i in range(0, len(terms) - 1, 2)]
        terms = pairs + terms[2 * len(pairs) :]
    return terms[0]


def factor_block(load, store):
    lane = lax.broadcasted_iota(jnp.int32, (8, NB), 1)
    sub = lax.broadcasted_iota(jnp.int32, (8, NB), 0)
    left = [load(i) for i in range(16)]
    right = [jnp.where(lane == sub + 8 * i, F32(1), F32(0)) for i in range(16)]

    def lanes(v, j):
        return jnp.broadcast_to(v[:, j : j + 1], (8, NB))

    def subs(v, s):
        return jnp.broadcast_to(v[s : s + 1, :], (8, NB))

    for b in range(16):
        more = b < 15
        c = [lanes(left[b], 8 * b + j) for j in range(8)]
        t = {(s, j): subs(c[j], s) for j in range(8) for s in range(j, 8)}
        va = [subs(left[b], s) for s in range(8)] if more else None
        vi = [subs(right[b], s) for s in range(8)]
        nx = [lanes(left[b + 1], 8 * b + j) for j in range(8)] if more else None
        r, d, m = [None] * 8, [None] * 8, {}
        for j in range(8):
            d[j] = t[j, j]
            r[j] = 1.0 / d[j]
            for s in range(j + 1, 8):
                m[s, j] = t[s, j] * r[j]
            for k in range(j + 1, 8):
                for s in range(k, 8):
                    t[s, k] = t[s, k] - m[s, j] * t[k, j]
            for s in range(j + 1, 8):
                if more:
                    va[s] = va[s] - m[s, j] * va[j]
                    nx[s] = nx[s] - m[s, j] * nx[j]
                vi[s] = vi[s] - m[s, j] * vi[j]
        if more:
            wa = [r[s] * va[s] for s in range(8)]
            wi = [r[s] * vi[s] for s in range(8)]
            next_left = left[b + 1] - total([nx[j] * wa[j] for j in range(8)])
            next_right = right[b + 1] - total([nx[j] * wi[j] for j in range(8)])
            for s in range(7, 0, -1):
                for j in range(s):
                    wa[j] = wa[j] - m[s, j] * wa[s]
                    wi[j] = wi[j] - m[s, j] * wi[s]
            for i in range(b + 2, 16):
                ci = [lanes(left[i], 8 * b + j) for j in range(8)]
                left[i] = left[i] - total([ci[j] * wa[j] for j in range(8)])
                right[i] = right[i] - total([ci[j] * wi[j] for j in range(8)])
            left[b + 1], right[b + 1] = next_left, next_right
        out = lax.rsqrt(d[0]) * vi[0]
        for s in range(1, 8):
            out = jnp.where(sub == s, lax.rsqrt(d[s]) * vi[s], out)
        store(b, out)


def identity(work):
    row = lax.broadcasted_iota(jnp.int32, (W, W), 0)
    col = lax.broadcasted_iota(jnp.int32, (W, W), 1)
    work[:, W:] = jnp.where(row == col, F32(1), F32(0))


def factor_steps(work, inv, first, last):
    def step(kb, carry):
        top = pl.multiple_of(kb * NB, NB)
        nxt = pl.multiple_of((kb + 1) * NB, NB)

        def load(i):
            return work[pl.ds(top + 8 * i, 8), pl.ds(top, NB)]

        def store(i, v):
            inv[8 * i : 8 * i + 8, :] = v

        factor_block(load, store)
        work[pl.ds(top, NB), pl.ds(nxt, W)] = dot(
            inv[...], work[pl.ds(top, NB), pl.ds(nxt, W)]
        )

        for k in range(W // NB - 1):

            @pl.when(kb == k)
            def _():
                rows, now = slice((k + 1) * NB, W), slice(k * NB, (k + 1) * NB)
                across = slice((k + 1) * NB, (k + 1) * NB + W)
                work[rows, across] -= dot(work[now, rows], work[now, across], 0, 0)

        return carry

    lax.fori_loop(first, last, step, 0)


def lay_out(work, cols, own, other, part):
    core = lax.axis_index("row") % 2
    for x in range(4):
        for y in range(4):
            for z in range(2):
                for source, k in ((own, core), (other, 1 - core)):
                    at = pl.multiple_of(8 * (16 * x + 8 * z + 2 * y + k), 8)
                    work[pl.ds(at, 8), cols] = source[4 * x + y, z, part]


def first_kernel(own, other, x0, work, inv):
    lay_out(work, slice(0, W), own, other, 0)
    identity(work)
    factor_steps(work, inv, 0, 4)
    x0[...] = work[:, W:]


def second_kernel(x0, own, other, u01, x1, work, inv):
    lay_out(work, slice(W, 2 * W), own, other, 0)
    lay_out(work, slice(0, W), own, other, 1)
    u01[...] = dot(x0[...], work[:, W:], 1, 1)
    work[:, :W] -= dot(u01[...], u01[...], 0, 0)
    identity(work)
    factor_steps(work, inv, 0, 4)
    x1[...] = work[:, W:]


def own_rows_kernel(x0, x1, u01, own, s1, s2, s3, b, g, a0, a1, sem):
    c = lax.axis_index("col")
    for dst, sources, k in ((a0, (own, s1, s2, s3), 0), (a1, (s1, own, s3, s2), 1)):
        for i, source in enumerate(sources):

            @pl.when(c == i)
            def _():
                pltpu.make_async_copy(source, dst, sem.at[k]).start()

        pltpu.make_async_copy(own, dst, sem.at[k]).wait()
    b0 = dot(a0[...], x0[...], 1, 1)
    b1 = dot(a1[...] - dot(b0, u01[...]), x1[...], 1, 1)
    g1 = dot(b1, x1[...])
    b[:, :W] = b0
    b[:, W:] = b1
    g[:, W:] = g1
    g[:, :W] = dot(b0 - dot(g1, u01[...], 1, 1), x0[...])


def thirds(v):
    high = v.astype(jnp.bfloat16)
    rest = v - high.astype(F32)
    mid = rest.astype(jnp.bfloat16)
    return high, mid, (rest - mid.astype(F32)).astype(jnp.bfloat16)


def bdot(a, b):
    return lax.dot_general(a, b, (((1,), (0,)), ((), ())), preferred_element_type=F32)


def last_kernel(slots, a, b, g, *rest):
    n = len(slots)
    bufs, out, (held, tile, parts, held_sem, in_sem, out_sem) = rest[:n], rest[n], rest[n + 1 :]
    r, c = lax.axis_index("row"), lax.axis_index("col")
    place = [
        [jnp.bitwise_xor(r, jnp.where((r + k) % 2 == 1, odd, even)) for even, odd, k in ids]
        for ids in slots
    ]

    def fetch(t, carry):
        columns = pl.ds(pl.multiple_of(1024 * t, 1024), 1024)
        for buf, rows in zip(bufs, place):
            for at, block in enumerate(rows):
                for l in range(2):
                    row = pl.multiple_of(8 * (64 * l + block), 8)
                    pltpu.make_async_copy(
                        buf.at[at, l, :, columns], held.at[t, pl.ds(row, 8)], held_sem.at[t]
                    ).start()
        pltpu.make_async_copy(a.at[:, t], tile.at[t], in_sem.at[t]).start()
        return carry

    lax.fori_loop(0, 4, fetch, 0)
    for k, v in enumerate(thirds(g[...])):
        parts[k] = v
    row = lax.broadcasted_iota(jnp.int32, (256, 128), 0)
    col = lax.broadcasted_iota(jnp.int32, (256, 128), 1)
    row_global = (row // 8) * W + r * 8 + row % 8

    def column(t, carry):
        pltpu.make_async_copy(held.at[t], held.at[t], held_sem.at[t]).wait()
        pltpu.make_async_copy(tile.at[t], tile.at[t], in_sem.at[t]).wait()
        flat = tile.at[t].reshape(2048, 128)

        def some(i, carry):
            high, mid, low = thirds(held[t, :, pl.ds(pl.multiple_of(512 * i, 512), 512)])
            product = (
                bdot(parts[0], low)
                + bdot(parts[2], high)
                + bdot(parts[1], mid)
                + bdot(parts[0], mid)
                + bdot(parts[1], high)
                + bdot(parts[0], high)
            )
            for k in range(4):
                m = 4 * i + k
                at = pl.ds(m, 256, stride=8)
                value = flat[at, :] - product[:, 128 * k : 128 * k + 128]
                trailing = (m > 0) | (c >= 2)
                flat[at, :] = jnp.where((row < 16) & trailing, F32(0), value)
            return carry

        lax.fori_loop(0, 2, some, 0)

        @pl.when(c < 2)
        def _():
            at = pl.ds(pl.multiple_of(128 * t, 128), 128)
            ahead = pl.ds(pl.multiple_of(W + 128 * t, 128), 128)
            first, second = b[:, at], b[:, ahead]
            mine = jnp.where(c == 0, first, second)
            flat[pl.ds(0, 256, stride=8), :] = jnp.where(
                row_global - c * W >= col + 128 * t, mine, F32(0)
            )

        pltpu.make_async_copy(tile.at[t], out.at[:, t], out_sem.at[t]).start()
        return carry

    lax.fori_loop(0, 4, column, 0)
    for t in range(4):
        pltpu.make_async_copy(tile.at[t], out.at[:, t], out_sem.at[t]).wait()


def steps(matrix):
    r = lax.axis_index("row")
    c = lax.axis_index("col")
    z_hi = (r // 8) % 2
    tiles = matrix.reshape(256, 8, 4, 128).transpose(0, 2, 1, 3)
    own = matrix[:, :, 0, :].reshape(256, W)

    def by_col(value):
        def send(*pairs):
            return lax.ppermute(value, "col", list(pairs))

        return send((0, 1), (1, 0)), send((0, 2), (1, 3)), send((0, 3), (1, 2))

    groups = [
        [q for q in range(64) if (q // 8) % 2 == z and q % 2 == k] for z in (0, 1) for k in (0, 1)
    ]

    def to_all(value):
        copies = jnp.broadcast_to(value, (16, *value.shape))
        return lax.all_to_all(
            copies, "row", split_axis=0, concat_axis=0, axis_index_groups=groups, tiled=True
        )

    head = matrix[:2, :, 0, :].reshape(16, W)
    s1, s2, s3 = by_col(head)
    d0 = jnp.where(c == 0, head, jnp.where(c == 1, s1, jnp.where(c == 2, s2, s3)))
    d1 = jnp.where(c == 1, head, jnp.where(c == 0, s1, jnp.where(c == 3, s2, s3)))
    mine = jnp.stack([d0[:8], d0[8:], d1[8:]])
    other = swap(mine, 8)
    both = jnp.where(z_hi == 0, jnp.stack([mine, other]), jnp.stack([other, mine]))
    d00 = to_all(both[:, :1])
    d00_other = swap(d00, 1)
    d1x = to_all(both[:, 1:])
    d1x_other = swap(d1x, 1)

    piece = tiles[:16].reshape(2, 8, 4096).reshape(1, 2, 8, 4096)
    t = jnp.concatenate([piece, swap(piece, 8)])
    a1, a2, a3 = by_col(own)
    n1 = swap(t, 2, 16)
    n3 = swap(t, 6, 48)
    n2 = swap(n3, 2, 16)
    t = jnp.concatenate([t, n1, n2, n3])
    m1 = swap(t, 16, 2)
    m3 = swap(t, 48, 6)
    m2 = swap(m3, 16, 2)
    bufs = [t, m1, m2, m3]
    for v in list(bufs):
        bufs.append(swap(v, 1))
    slots = [
        [(16 * p + 2 * q + z + k, 16 * q + 2 * p + z + k, k) for q in range(4) for z in (0, 8)]
        for k in (0, 1)
        for p in range(4)
    ]

    square = jax.ShapeDtypeStruct((W, W), F32)
    wide = jax.ShapeDtypeStruct((256, 2 * W), F32)
    scratch = [pltpu.VMEM((W, 2 * W), F32), pltpu.VMEM((NB, NB), F32)]
    x0 = pl.pallas_call(
        first_kernel, out_shape=square, in_specs=[VM] * 2, out_specs=VM, scratch_shapes=scratch
    )(d00, d00_other)
    u01, x1 = pl.pallas_call(
        second_kernel,
        out_shape=[square, square],
        in_specs=[VM] * 3,
        out_specs=[VM] * 2,
        scratch_shapes=scratch,
    )(x0, d1x, d1x_other)
    b, g = pl.pallas_call(
        own_rows_kernel,
        out_shape=[wide, wide],
        in_specs=[VM] * 3 + [ANY] * 4,
        out_specs=[VM] * 2,
        scratch_shapes=[
            pltpu.VMEM((256, W), F32),
            pltpu.VMEM((256, W), F32),
            pltpu.SemaphoreType.DMA((2,)),
        ],
    )(x0, x1, u01, own, a1, a2, a3)
    result = pl.pallas_call(
        functools.partial(last_kernel, slots),
        out_shape=jax.ShapeDtypeStruct((256, 4, 8, 128), F32),
        in_specs=[ANY, VM, VM] + [ANY] * len(bufs),
        out_specs=ANY,
        scratch_shapes=[
            pltpu.VMEM((4, 1024, 1024), F32),
            pltpu.VMEM((4, 256, 8, 128), F32),
            pltpu.VMEM((3, 256, 1024), jnp.bfloat16),
            pltpu.SemaphoreType.DMA((4,)),
            pltpu.SemaphoreType.DMA((4,)),
            pltpu.SemaphoreType.DMA((4,)),
        ],
    )(tiles, b, g, *bufs)
    return result.transpose(0, 2, 1, 3).reshape(matrix.shape)


def solution(mesh):
    return jax.shard_map(
        steps,
        mesh=mesh,
        in_specs=(P(None, "row", None, "col"),),
        out_specs=P(None, "row", None, "col"),
        check_vma=False,
    )
```

```python
import functools

import jax
import jax.numpy as jnp
from jax import lax
from jax.experimental import pallas as pl
from jax.experimental.pallas import tpu as pltpu
from jax.sharding import PartitionSpec as P


W = 512
H = W // 2
NB = 128
F32 = jnp.float32
HI = lax.Precision.HIGHEST
ANY = pl.BlockSpec(memory_space=pl.ANY)
VM = pl.BlockSpec(memory_space=pltpu.VMEM)


def swap(value, mask, mask_odd=None):
    mask_odd = mask if mask_odd is None else mask_odd
    pairs = [(r, r ^ (mask_odd if r & 1 else mask)) for r in range(64)]
    return lax.ppermute(value, "row", pairs)


def dot(a, b, da=1, db=0):
    return lax.dot_general(
        a, b, (((da,), (db,)), ((), ())), precision=HI, preferred_element_type=F32
    )


def total(terms):
    while len(terms) > 1:
        pairs = [terms[i] + terms[i + 1] for i in range(0, len(terms) - 1, 2)]
        terms = pairs + terms[2 * len(pairs) :]
    return terms[0]


def factor_block(load, store):
    lane = lax.broadcasted_iota(jnp.int32, (8, NB), 1)
    sub = lax.broadcasted_iota(jnp.int32, (8, NB), 0)
    left = [load(i) for i in range(16)]
    right = [jnp.where(lane == sub + 8 * i, F32(1), F32(0)) for i in range(16)]

    def lanes(v, j):
        return jnp.broadcast_to(v[:, j : j + 1], (8, NB))

    def subs(v, s):
        return jnp.broadcast_to(v[s : s + 1, :], (8, NB))

    for b in range(16):
        more = b < 15
        c = [lanes(left[b], 8 * b + j) for j in range(8)]
        t = {(s, j): subs(c[j], s) for j in range(8) for s in range(j, 8)}
        va = [subs(left[b], s) for s in range(8)] if more else None
        vi = [subs(right[b], s) for s in range(8)]
        nx = [lanes(left[b + 1], 8 * b + j) for j in range(8)] if more else None
        r, d, m = [None] * 8, [None] * 8, {}
        for j in range(8):
            d[j] = t[j, j]
            r[j] = 1.0 / d[j]
            for s in range(j + 1, 8):
                m[s, j] = t[s, j] * r[j]
            for k in range(j + 1, 8):
                for s in range(k, 8):
                    t[s, k] = t[s, k] - m[s, j] * t[k, j]
            for s in range(j + 1, 8):
                if more:
                    va[s] = va[s] - m[s, j] * va[j]
                    nx[s] = nx[s] - m[s, j] * nx[j]
                vi[s] = vi[s] - m[s, j] * vi[j]
        if more:
            wa = [r[s] * va[s] for s in range(8)]
            wi = [r[s] * vi[s] for s in range(8)]
            next_left = left[b + 1] - total([nx[j] * wa[j] for j in range(8)])
            next_right = right[b + 1] - total([nx[j] * wi[j] for j in range(8)])
            for s in range(7, 0, -1):
                for j in range(s):
                    wa[j] = wa[j] - m[s, j] * wa[s]
                    wi[j] = wi[j] - m[s, j] * wi[s]
            for i in range(b + 2, 16):
                ci = [lanes(left[i], 8 * b + j) for j in range(8)]
                left[i] = left[i] - total([ci[j] * wa[j] for j in range(8)])
                right[i] = right[i] - total([ci[j] * wi[j] for j in range(8)])
            left[b + 1], right[b + 1] = next_left, next_right
        out = lax.rsqrt(d[0]) * vi[0]
        for s in range(1, 8):
            out = jnp.where(sub == s, lax.rsqrt(d[s]) * vi[s], out)
        store(b, out)


def identity(work):
    row = lax.broadcasted_iota(jnp.int32, (W, W), 0)
    col = lax.broadcasted_iota(jnp.int32, (W, W), 1)
    work[:, W:] = jnp.where(row == col, F32(1), F32(0))


def factor_steps(work, inv, first, last):
    def step(kb, carry):
        top = pl.multiple_of(kb * NB, NB)
        nxt = pl.multiple_of((kb + 1) * NB, NB)

        def load(i):
            return work[pl.ds(top + 8 * i, 8), pl.ds(top, NB)]

        def store(i, v):
            inv[8 * i : 8 * i + 8, :] = v

        factor_block(load, store)
        work[pl.ds(top, NB), pl.ds(nxt, W)] = dot(
            inv[...], work[pl.ds(top, NB), pl.ds(nxt, W)]
        )

        for k in range(W // NB - 1):

            @pl.when(kb == k)
            def _():
                rows, now = slice((k + 1) * NB, W), slice(k * NB, (k + 1) * NB)
                across = slice((k + 1) * NB, (k + 1) * NB + W)
                work[rows, across] -= dot(work[now, rows], work[now, across], 0, 0)

        return carry

    lax.fori_loop(first, last, step, 0)


def lay_out(work, cols, own, other, part):
    core = lax.axis_index("row") % 2
    for x in range(4):
        for y in range(4):
            for z in range(2):
                for source, k in ((own, core), (other, 1 - core)):
                    at = pl.multiple_of(8 * (16 * x + 8 * z + 2 * y + k), 8)
                    work[pl.ds(at, 8), cols] = source[4 * x + y, z, part]


def first_kernel(own, other, x0, work, inv):
    lay_out(work, slice(0, W), own, other, 0)
    identity(work)
    factor_steps(work, inv, 0, 4)
    x0[...] = work[:, W:]


def second_kernel(x0, own, other, u01, x1, work, inv):
    lay_out(work, slice(W, 2 * W), own, other, 0)
    lay_out(work, slice(0, W), own, other, 1)
    u01[:H, :] = dot(x0[:H, :H], work[:, W : W + H], 1, 1)
    u01[H:, :] = dot(x0[H:, :], work[:, W:], 1, 1)
    work[:H, :W] -= dot(u01[:, :H], u01[...], 0, 0)
    work[H:, H:W] -= dot(u01[:, H:], u01[:, H:], 0, 0)
    identity(work)
    factor_steps(work, inv, 0, 4)
    x1[...] = work[:, W:]


def times_inverse_t(a, x):
    return jnp.concatenate([dot(a[:, :H], x[:H, :H], 1, 1), dot(a, x[H:, :], 1, 1)], axis=1)


def times_inverse(a, x):
    return jnp.concatenate([dot(a, x[:, :H]), dot(a[:, H:], x[H:, H:])], axis=1)


def own_rows_kernel(x0, x1, u01, own, s1, s2, s3, b, g, a0, a1, sem):
    c = lax.axis_index("col")
    for dst, sources, k in ((a0, (own, s1, s2, s3), 0), (a1, (s1, own, s3, s2), 1)):
        for i, source in enumerate(sources):

            @pl.when(c == i)
            def _():
                pltpu.make_async_copy(source, dst, sem.at[k]).start()

    pltpu.make_async_copy(own, a0, sem.at[0]).wait()
    b0 = times_inverse_t(a0[...], x0)
    pltpu.make_async_copy(own, a1, sem.at[1]).wait()
    b1 = times_inverse_t(a1[...] - dot(b0, u01[...]), x1)
    g1 = times_inverse(b1, x1)
    b[:, :W] = b0
    b[:, W:] = b1
    g[:, W:] = g1
    g[:, :W] = times_inverse(b0 - dot(g1, u01[...], 1, 1), x0)


def thirds(v):
    high = v.astype(jnp.bfloat16)
    rest = v - high.astype(F32)
    mid = rest.astype(jnp.bfloat16)
    return high, mid, (rest - mid.astype(F32)).astype(jnp.bfloat16)


def bdot(a, b):
    return lax.dot_general(a, b, (((1,), (0,)), ((), ())), preferred_element_type=F32)


def last_kernel(slots, a, b, g, *rest):
    n = len(slots)
    bufs, out, (held, tile, parts, held_sem, in_sem, out_sem) = rest[:n], rest[n], rest[n + 1 :]
    r, c = lax.axis_index("row"), lax.axis_index("col")
    place = [
        [jnp.bitwise_xor(r, jnp.where((r + k) % 2 == 1, odd, even)) for even, odd, k in ids]
        for ids in slots
    ]

    def fetch(t, carry):
        columns = pl.ds(pl.multiple_of(1024 * t, 1024), 1024)
        for buf, rows in zip(bufs, place):
            for at, block in enumerate(rows):
                for l in range(2):
                    row = pl.multiple_of(8 * (64 * l + block), 8)
                    pltpu.make_async_copy(
                        buf.at[at, l, :, columns], held.at[t, pl.ds(row, 8)], held_sem.at[t]
                    ).start()
        pltpu.make_async_copy(a.at[:, t], tile.at[t], in_sem.at[t]).start()
        return carry

    lax.fori_loop(0, 4, fetch, 0)
    for k, v in enumerate(thirds(g[...])):
        parts[k] = v
    row = lax.broadcasted_iota(jnp.int32, (256, 128), 0)
    col = lax.broadcasted_iota(jnp.int32, (256, 128), 1)
    row_global = (row // 8) * W + r * 8 + row % 8

    def column(t, carry):
        pltpu.make_async_copy(held.at[t], held.at[t], held_sem.at[t]).wait()
        pltpu.make_async_copy(tile.at[t], tile.at[t], in_sem.at[t]).wait()
        flat = tile.at[t].reshape(2048, 128)

        def some(i, carry):
            high, mid, low = thirds(held[t, :, pl.ds(pl.multiple_of(512 * i, 512), 512)])
            product = (
                bdot(parts[0], low)
                + bdot(parts[2], high)
                + bdot(parts[1], mid)
                + bdot(parts[0], mid)
                + bdot(parts[1], high)
                + bdot(parts[0], high)
            )
            for k in range(4):
                m = 4 * i + k
                at = pl.ds(m, 256, stride=8)
                value = flat[at, :] - product[:, 128 * k : 128 * k + 128]
                trailing = (m > 0) | (c >= 2)
                flat[at, :] = jnp.where((row < 16) & trailing, F32(0), value)
            return carry

        lax.fori_loop(0, 2, some, 0, unroll=2)

        @pl.when(c < 2)
        def _():
            at = pl.ds(pl.multiple_of(128 * t, 128), 128)
            ahead = pl.ds(pl.multiple_of(W + 128 * t, 128), 128)
            first, second = b[:, at], b[:, ahead]
            mine = jnp.where(c == 0, first, second)
            flat[pl.ds(0, 256, stride=8), :] = jnp.where(
                row_global - c * W >= col + 128 * t, mine, F32(0)
            )

        pltpu.make_async_copy(tile.at[t], out.at[:, t], out_sem.at[t]).start()
        return carry

    lax.fori_loop(0, 4, column, 0)
    for t in range(4):
        pltpu.make_async_copy(tile.at[t], out.at[:, t], out_sem.at[t]).wait()


def steps(matrix):
    r = lax.axis_index("row")
    c = lax.axis_index("col")
    z_hi = (r // 8) % 2
    tiles = matrix.reshape(256, 8, 4, 128).transpose(0, 2, 1, 3)
    own = matrix[:, :, 0, :].reshape(256, W)

    def by_col(value):
        def send(*pairs):
            return lax.ppermute(value, "col", list(pairs))

        return send((0, 1), (1, 0)), send((0, 2), (1, 3)), send((0, 3), (1, 2))

    groups = [
        [q for q in range(64) if (q // 8) % 2 == z and q % 2 == k] for z in (0, 1) for k in (0, 1)
    ]

    def to_all(value):
        copies = jnp.broadcast_to(value, (16, *value.shape))
        return lax.all_to_all(
            copies, "row", split_axis=0, concat_axis=0, axis_index_groups=groups, tiled=True
        )

    head = matrix[:2, :, 0, :].reshape(16, W)
    s1, s2, s3 = by_col(head)
    d0 = jnp.where(c == 0, head, jnp.where(c == 1, s1, jnp.where(c == 2, s2, s3)))
    d1 = jnp.where(c == 1, head, jnp.where(c == 0, s1, jnp.where(c == 3, s2, s3)))
    mine = jnp.stack([d0[:8], d0[8:], d1[8:]])
    other = swap(mine, 8)
    both = jnp.where(z_hi == 0, jnp.stack([mine, other]), jnp.stack([other, mine]))
    d00 = to_all(both[:, :1])
    d00_other = swap(d00, 1)
    d1x = to_all(both[:, 1:])
    d1x_other = swap(d1x, 1)

    piece = tiles[:16].reshape(2, 8, 4096).reshape(1, 2, 8, 4096)
    t = jnp.concatenate([piece, swap(piece, 8)])
    a1, a2, a3 = by_col(own)
    n1 = swap(t, 2, 16)
    n3 = swap(t, 6, 48)
    n2 = swap(n3, 2, 16)
    t = jnp.concatenate([t, n1, n2, n3])
    m1 = swap(t, 16, 2)
    m3 = swap(t, 48, 6)
    m2 = swap(m3, 16, 2)
    bufs = [t, m1, m2, m3]
    for v in list(bufs):
        bufs.append(swap(v, 1))
    slots = [
        [(16 * p + 2 * q + z + k, 16 * q + 2 * p + z + k, k) for q in range(4) for z in (0, 8)]
        for k in (0, 1)
        for p in range(4)
    ]

    square = jax.ShapeDtypeStruct((W, W), F32)
    wide = jax.ShapeDtypeStruct((256, 2 * W), F32)
    scratch = [pltpu.VMEM((W, 2 * W), F32), pltpu.VMEM((NB, NB), F32)]
    x0 = pl.pallas_call(
        first_kernel, out_shape=square, in_specs=[VM] * 2, out_specs=VM, scratch_shapes=scratch
    )(d00, d00_other)
    u01, x1 = pl.pallas_call(
        second_kernel,
        out_shape=[square, square],
        in_specs=[VM] * 3,
        out_specs=[VM] * 2,
        scratch_shapes=scratch,
    )(x0, d1x, d1x_other)
    b, g = pl.pallas_call(
        own_rows_kernel,
        out_shape=[wide, wide],
        in_specs=[VM] * 3 + [ANY] * 4,
        out_specs=[VM] * 2,
        scratch_shapes=[
            pltpu.VMEM((256, W), F32),
            pltpu.VMEM((256, W), F32),
            pltpu.SemaphoreType.DMA((2,)),
        ],
    )(x0, x1, u01, own, a1, a2, a3)
    result = pl.pallas_call(
        functools.partial(last_kernel, slots),
        out_shape=jax.ShapeDtypeStruct((256, 4, 8, 128), F32),
        in_specs=[ANY, VM, VM] + [ANY] * len(bufs),
        out_specs=ANY,
        scratch_shapes=[
            pltpu.VMEM((4, 1024, 1024), F32),
            pltpu.VMEM((4, 256, 8, 128), F32),
            pltpu.VMEM((3, 256, 1024), jnp.bfloat16),
            pltpu.SemaphoreType.DMA((4,)),
            pltpu.SemaphoreType.DMA((4,)),
            pltpu.SemaphoreType.DMA((4,)),
        ],
    )(tiles, b, g, *bufs)
    return result.transpose(0, 2, 1, 3).reshape(matrix.shape)


def solution(mesh):
    return jax.shard_map(
        steps,
        mesh=mesh,
        in_specs=(P(None, "row", None, "col"),),
        out_specs=P(None, "row", None, "col"),
        check_vma=False,
    )
```
